32 devices in a mesh: vox: 4 (over x, core), mem: 8 (over z, y).
Axes of the slice: x: 2, y: 2, z: 4, core: 2. Of those that a mesh axis runs over, the one named last changes fastest.
Arguments:
- ensemble: bfloat16 [256, 65536], P('mem', 'vox'), may hold values from -6 to 6
- partials: float32 [4, 256, 16384], P('vox', 'mem'), may hold values from -6 to 6
- perturb: float32 [256, 16384], P('mem', 'vox'), may hold values from -6 to 6
- observed: float32 [16384], P('vox'), may hold values from -6 to 6
- variance: float32 [16384], P('vox'), may hold values from 0.5 to 2
- obs_lists: int32 [512, 16], P(('vox', 'mem')), may hold values from 0 to 31, all different within a row
- taper_index: int32 [512, 16], P(('vox', 'mem')), may hold values from 0 to 15
- taper_table: float32 [16], replicated, may hold values from 0.1 to 1
Outputs:
- updated: bfloat16 [256, 65536], P('mem', 'vox')
The draws below stay inside these ranges and needn't reach their ends.
All inputs are finite; a program needn't handle non-finite values.
Results may differ from the reference program's by a relative error of at most 0.017.
Values may be sent and summed in bfloat16 or wider, within the bound.
No kernel may reach another device: no remote copies, remote signals or barrier semaphores. Data moves between devices by JAX's collectives and lax.ppermute only.
A program may use at most 128 MiB of HBM per device.

```python
import math
import jax
import jax.numpy as jnp
from jax import lax

K = 256
BS = 128
OB = 128
NT = 16
OBG = 32
L = 16
NOBS = 16384
NBLK = 512
NCELL = 65536
N_VOX = 4


def place_ends(values, stream_key, low, largest):
    extent = values.shape
    place = [jax.random.randint(jax.random.fold_in(stream_key, axis), (), 0, extent[axis]) for axis in range(len(extent))]
    values = values.at[tuple(place)].set(low)
    longest = extent.index(max(extent))
    place[longest] = (place[longest] + 1) % extent[longest]
    return values.at[tuple(place)].set(largest)


def spiked(drawn, stream_key, source, target, blocks, factor):
    owner, partner = [(jnp.arange(drawn.shape[position]) // (drawn.shape[position] // blocks)).reshape([-1 if axis == position else 1 for axis in range(drawn.ndim)]) for position in (source, target)]
    chosen = jax.random.permutation(stream_key, blocks)[partner]
    strong = (owner == chosen) | (owner == (partner + blocks // 2) % blocks)
    return jnp.where(strong, factor * drawn, drawn)


def levels(own_key, shape, cuts, low, largest):
    gain, own = 1.0, jax.random.fold_in(own_key, 6)
    for dim, blocks in cuts:
        draws = jnp.exp(jax.random.uniform(jax.random.fold_in(own, dim), (blocks,), jnp.float32, low / len(cuts), largest / len(cuts)))
        gain = gain * jnp.repeat(draws, shape[dim] // blocks).reshape([-1 if axis == dim else 1 for axis in range(len(shape))])
    return gain


def distinct(rng, rows, amount, top, lift):
    order = jax.random.permutation(jax.random.fold_in(rng, 1), amount)
    boost = order
    for power in range(3):
        boost = boost * boost // amount
    boost = boost * lift // amount
    chance = jax.random.randint(jax.random.fold_in(rng, 2), (rows, amount), 0, 4096) + boost
    holders = jax.random.permutation(jax.random.fold_in(rng, 3), rows)[jnp.arange(amount) % rows]
    chance = jnp.where(jnp.arange(rows)[:, None] == holders[None, :], 1 << 14, chance)
    priority = chance * amount + jnp.arange(amount)
    return lax.top_k(priority.astype(jnp.int32), top)[1].astype(jnp.int32)


def centred(own_key, dims, spread, limit, split=(), held_as=jnp.bfloat16):
    gain = levels(own_key, dims, split, -0.22, 0.18) if split else 1.0
    values = jax.random.normal(own_key, dims, jnp.float32) * spread * gain
    return jnp.minimum(jnp.maximum(values, -limit), limit).astype(held_as)


def bell_draw_with(stream_key, shape, deviation, limit, cuts, heavy, kind=jnp.bfloat16):
    values = deviation * jax.random.normal(stream_key, shape, jnp.float32)
    if cuts:
        values = values * levels(stream_key, shape, cuts, -0.22, 0.18)
    return jnp.clip(spiked(values, jax.random.fold_in(stream_key, 3), *heavy), -limit, limit).astype(kind)


def setup_inputs(seed: int = 0) -> dict:
    arg_keys = jax.random.split(jax.random.key(seed), 9)
    ensemble = centred(arg_keys[0], (K, NCELL), 1.0, 6.0, ((0, 8), (1, 4)))
    partials = bell_draw_with(arg_keys[1], (N_VOX, K, NOBS), 0.35, 6.0, ((0, 4), (1, 8)), (0, 2, 4, 2.0), jnp.float32)
    perturb = centred(arg_keys[2], (K, NOBS), 0.5, 6.0, ((0, 8), (1, 4)), jnp.float32)
    observed = centred(arg_keys[3], (NOBS,), 1.0, 6.0, ((0, 4),), jnp.float32)
    variance = jnp.clip(jnp.exp(math.log(2.0) - 1.3862944 * jax.random.uniform(arg_keys[4], (NOBS,), jnp.float32) ** levels(arg_keys[4], (NOBS,), ((0, 4),), -0.2, 0.2)), 0.5, 2.0)
    obs_lists = distinct(arg_keys[5], NBLK, OBG, L, 0)
    taper_index = place_ends(jax.random.randint(arg_keys[6], (NBLK, L), 0, NT), jax.random.fold_in(arg_keys[6], 1), 0, NT - 1).astype(jnp.int32)
    taper_table = jnp.clip(jax.random.uniform(arg_keys[7], (NT,), jnp.float32, 0.1, 1.0), 0.1, 1.0)
    return dict(ensemble=ensemble, partials=partials, perturb=perturb, observed=observed, variance=variance, obs_lists=obs_lists, taper_index=taper_index, taper_table=taper_table)


def reference(ensemble, partials, perturb, observed, variance, obs_lists, taper_index, taper_table):
    high = lax.Precision.HIGHEST
    predicted = jnp.sum(partials, axis=0).astype(jnp.bfloat16)
    pred_f = predicted.astype(jnp.float32)
    weights = ((observed[None, :] + perturb - pred_f) / variance[None, :]).astype(jnp.bfloat16)
    obs_anom = (pred_f - jnp.mean(pred_f, axis=0, keepdims=True)).astype(jnp.bfloat16)
    state_f = ensemble.astype(jnp.float32)
    state_anom = (state_f - jnp.mean(state_f, axis=0, keepdims=True)).astype(jnp.bfloat16)
    tapers = taper_table[taper_index]
    picks = (obs_lists[:, :, None] == jnp.arange(OBG, dtype=jnp.int32)[None, None, :]).astype(jnp.float32)
    coeff = jnp.sum(tapers[:, :, None] * picks, axis=1)
    group_obs = OBG * OB
    group_blocks = NBLK // N_VOX

    def one_group(g):
        start = (g * group_obs).astype(jnp.int32)
        yc = lax.dynamic_slice_in_dim(obs_anom, start, group_obs, 1).reshape(K, OBG, OB).astype(jnp.float32)
        wt = lax.dynamic_slice_in_dim(weights, start, group_obs, 1).reshape(K, OBG, OB).astype(jnp.float32)
        moments = jnp.einsum("kbi,lbi->bkl", yc, wt, precision=high)
        cg = lax.dynamic_slice_in_dim(coeff, (g * group_blocks).astype(jnp.int32), group_blocks, 0)
        combined = jnp.einsum("bo,okl->bkl", cg, moments, precision=high).astype(jnp.bfloat16)
        cstart = (g * group_blocks * BS).astype(jnp.int32)
        xa = lax.dynamic_slice_in_dim(state_anom, cstart, group_blocks * BS, 1).reshape(K, group_blocks, BS).astype(jnp.float32)
        xo = lax.dynamic_slice_in_dim(state_f, cstart, group_blocks * BS, 1)
        increment = jnp.einsum("kbc,bkl->lbc", xa, combined.astype(jnp.float32), precision=high).reshape(K, group_blocks * BS)
        return (xo + increment * (1.0 / (K - 1))).astype(jnp.bfloat16)

    result = lax.map(one_group, jnp.arange(N_VOX, dtype=jnp.int32))
    return jnp.transpose(result, (1, 0, 2)).reshape(K, NCELL)
```

```python
import functools

import jax
import jax.numpy as jnp
from jax import lax
from jax.experimental import pallas as pl
from jax.experimental.pallas import tpu as pltpu
from jax.sharding import PartitionSpec as P

OB = 128
SUB = 8
AXES = ("vox", "mem")
BF = jnp.bfloat16
F32 = jnp.float32


class Plan:
    def __init__(self, nv, nm):
        assert nv % 2 == 0 and nm % nv == 0
        self.nv, self.nm = nv, nm
        self.half, self.inner = nv // 2, nm // nv
        self.chips = nm // 2
        self.everyone = [(v, m) for v in range(nv) for m in range(nm)]

    def device(self, v, q, h):
        x, c = divmod(v, 2)
        qx, qy = divmod(q, self.inner)
        return ((qx + x) % self.half) * 2 + h, (c * self.half + x) * self.inner + qy

    def moved(self, q, i):
        ix, iy = divmod(i, self.inner)
        return ((q // self.inner + ix) % self.half) * self.inner + (q % self.inner + iy) % self.inner

    def flat(self, pairs):
        return [(a * self.nm + b, c * self.nm + d) for (a, b), (c, d) in pairs]

    def out_to_plane(self, i):
        return self.flat([((v, m), self.device(v, self.moved(m // 2, i), m % 2)) for v, m in self.everyone])

    def back(self, i):
        return [(b, a) for a, b in self.out_to_plane(i)]

    def in_plane(self, i):
        return self.flat(
            [
                (self.device(v, q, h), self.device(v, self.moved(q, i), h))
                for v in range(self.nv)
                for q in range(self.chips)
                for h in range(2)
            ]
        )

    def core(self):
        return self.flat([((v, m), (v ^ 1, m)) for v, m in self.everyone])

    def x_shift(self, s):
        return self.flat([((v, m), ((v + 2 * s) % self.nv, m)) for v, m in self.everyone])


def cost(flops, moved):
    return pl.CostEstimate(flops=flops, bytes_accessed=moved, transcendentals=0)


def vmem(count):
    return [pl.BlockSpec(memory_space=pltpu.VMEM)] * count


def center_kernel(parts, *refs):
    out = refs[parts]
    width = out.shape[1]
    rows = refs[0].shape[0]

    def step(t, carry):
        cols = pl.ds(pl.multiple_of(t * OB, OB), OB)
        values = [r[:, cols].astype(F32) for r in refs[:parts]]
        mean = sum(jnp.sum(x, axis=0, keepdims=True) for x in values) * (1.0 / (parts * rows))
        out[:, cols] = jnp.concatenate([x - mean for x in values], axis=0).astype(BF)
        return carry

    lax.fori_loop(0, width // OB, step, 0)


def center_state(pieces):
    rows, width = pieces[0].shape
    total = rows * len(pieces)
    return pl.pallas_call(
        functools.partial(center_kernel, len(pieces)),
        out_shape=jax.ShapeDtypeStruct((total, width), BF),
        in_specs=vmem(len(pieces)),
        out_specs=vmem(1)[0],
        cost_estimate=cost(4 * total * width, 4 * total * width),
        name="center_state",
    )(*pieces)


def update_kernel(own_parts, *refs):
    n = own_parts
    own, other, pert, state = refs[:n], refs[n : 2 * n], refs[2 * n : 3 * n], refs[3 * n : 4 * n]
    obs, var, kron, anom = refs[4 * n : 4 * n + 4]
    outs = refs[4 * n + 4 : 5 * n + 4]
    stacked, combined = refs[5 * n + 4 :]
    rows = own[0].shape[0]
    count = 2 * n * rows
    lanes = n * rows
    tiles = lanes // SUB
    groups = own[0].shape[1] // OB
    blocks = combined.shape[0]

    def moment(o, carry):
        cols = pl.ds(pl.multiple_of(o * OB, OB), OB)
        mine = jnp.concatenate([r[:, cols].astype(F32) for r in own], axis=0)
        theirs = jnp.concatenate([r[:, cols].astype(F32) for r in other], axis=0)
        noise = jnp.concatenate([r[:, cols].astype(F32) for r in pert], axis=0)
        mean = (jnp.sum(mine, axis=0, keepdims=True) + jnp.sum(theirs, axis=0, keepdims=True)) * (1.0 / count)
        weights = ((obs[:, cols] + noise - mine) / var[:, cols]).astype(BF)
        anomaly = jnp.concatenate([mine - mean, theirs - mean], axis=0).astype(BF)
        m = lax.dot_general(weights, anomaly, (((1,), (1,)), ((), ())), preferred_element_type=F32)
        stacked[:, pl.ds(pl.multiple_of(o * SUB, SUB), SUB), :] = m.reshape(tiles, SUB, count)
        return carry

    lax.fori_loop(0, groups, moment, 0)

    def combine(g, carry):
        c = lax.dot_general(
            kron[...], stacked[g].astype(BF), (((1,), (0,)), ((), ())), preferred_element_type=F32
        )
        combined[:, pl.ds(pl.multiple_of(g * SUB, SUB), SUB), :] = c.reshape(blocks, SUB, count)
        return carry

    lax.fori_loop(0, tiles, combine, 0)

    cells = anom.shape[1] // blocks

    def increment(b, carry):
        cols = pl.ds(pl.multiple_of(b * cells, cells), cells)
        inc = lax.dot_general(
            combined[b].astype(BF), anom[:, cols], (((1,), (0,)), ((), ())), preferred_element_type=F32
        )
        for i in range(n):
            new = state[i][:, cols].astype(F32) + inc[i * rows : (i + 1) * rows, :] * (1.0 / (count - 1))
            outs[i][:, cols] = new.astype(BF)
        return carry

    lax.fori_loop(0, blocks, increment, 0)


def update(own, other, pert, state, obs, var, kron, anom, blocks):
    n = len(own)
    rows, data = own[0].shape
    cells = state[0].shape[1]
    count, lanes = 2 * n * rows, n * rows
    groups = data // OB
    flops = 2 * lanes * count * (data + kron.shape[0] * groups * SUB // SUB + cells)
    return pl.pallas_call(
        functools.partial(update_kernel, n),
        out_shape=[jax.ShapeDtypeStruct((rows, cells), BF)] * n,
        in_specs=vmem(4 * n + 4),
        out_specs=vmem(n),
        scratch_shapes=[
            pltpu.VMEM((lanes // SUB, groups * SUB, count), F32),
            pltpu.VMEM((blocks, lanes, count), F32),
        ],
        cost_estimate=cost(flops, 2 * (3 * lanes * data + 3 * count * cells)),
        compiler_params=pltpu.CompilerParams(vmem_limit_bytes=60 << 20),
        name="update",
    )(*own, *other, *pert, *state, obs, var, kron, anom)


def place_kernel(parts, at, *refs):
    out, sems = refs[parts], refs[parts + 1]
    width = refs[0].shape[1]
    copies = []
    for i in range(parts):
        start = pl.multiple_of(at[i] * width, OB)
        copies.append(pltpu.make_async_copy(refs[i], out.at[:, pl.ds(start, width)], sems.at[i]))
    for c in copies:
        c.start()
    for c in copies:
        c.wait()


def place(pieces, at):
    n = len(pieces)
    rows, width = pieces[0].shape
    return pl.pallas_call(
        functools.partial(place_kernel, n),
        grid_spec=pltpu.PrefetchScalarGridSpec(
            num_scalar_prefetch=1,
            in_specs=vmem(n),
            out_specs=pl.BlockSpec(memory_space=pl.ANY),
            scratch_shapes=[pltpu.SemaphoreType.DMA((n,))],
        ),
        out_shape=jax.ShapeDtypeStruct((rows, n * width), BF),
        cost_estimate=cost(0, 4 * n * rows * width),
        name="place",
    )(at, *pieces)


def local(plan, ensemble, partials, perturb, observed, variance, obs_lists, taper_index, taper_table):
    n, half = plan.chips, plan.half
    v, m = lax.axis_index("vox"), lax.axis_index("mem")
    x, core = v // 2, v % 2
    rows, data = perturb.shape
    per_chip = ensemble.shape[1] // n

    def send(value, pairs):
        return lax.ppermute(value, AXES, pairs)

    parts = partials[0].reshape(rows, half, 2, data)
    away = lax.dynamic_slice_in_dim(parts, 1 - core, 1, 2)[:, :, 0].astype(BF)
    got = send(away, plan.core())
    pair = lax.dynamic_slice_in_dim(parts, core, 1, 2)[:, :, 0] + got.astype(F32)
    total = lax.dynamic_slice_in_dim(pair, x, 1, 1)[:, 0]
    for s in range(1, half):
        piece = lax.dynamic_slice_in_dim(pair, (x + s) % half, 1, 1)[:, 0].astype(BF)
        total = total + send(piece, plan.x_shift(s)).astype(F32)
    predicted = total.astype(BF)

    groups = data // OB
    table_hits = (
        taper_index[:, :, None] == jnp.arange(taper_table.shape[0], dtype=jnp.int32)[None, None, :]
    ).astype(F32)
    tapers = jnp.sum(table_hits * taper_table[None, None, :], axis=2)
    picks = (obs_lists[:, :, None] == jnp.arange(groups, dtype=jnp.int32)[None, None, :]).astype(F32)
    coeff = jnp.sum(tapers[:, :, None] * picks, axis=1)
    own_blocks = coeff.shape[0]
    first = plan.out_to_plane(0)
    small = send(jnp.concatenate([observed, variance, coeff.reshape(-1)]), first)
    obs, var = small[:data].reshape(1, data), small[data : 2 * data].reshape(1, data)
    mine = small[2 * data :]
    theirs = send(mine, plan.core())
    coeff = jnp.where(core == 0, jnp.concatenate([mine, theirs]), jnp.concatenate([theirs, mine]))
    blocks = 2 * own_blocks
    coeff = coeff.reshape(blocks, groups)
    kron = (coeff[:, None, :, None] * jnp.eye(SUB, dtype=F32)[None, :, None, :]).astype(BF)
    kron = kron.reshape(blocks * SUB, groups * SUB)

    def chip(i):
        return plan.moved(m // 2, i)

    own_state = [
        send(lax.dynamic_slice_in_dim(ensemble, chip(i) * per_chip, per_chip, 1), plan.out_to_plane(i))
        for i in range(n)
    ]
    other_state = [send(s, plan.core()) for s in own_state]
    anom = center_state(own_state + other_state)

    noise = send(perturb.astype(BF), first)
    pert = [noise] + [send(noise, plan.in_plane(i)) for i in range(1, n)]
    arrived = send(predicted, first)
    own = [arrived] + [send(arrived, plan.in_plane(i)) for i in range(1, n)]
    other = [send(p, plan.core()) for p in own]

    new = update(own, other, pert, own_state, obs, var, kron, anom, blocks)
    back = [send(new[i], plan.back(i)) for i in range(n)]
    at = jnp.stack([chip(i) for i in range(n)]).astype(jnp.int32)
    return place(back, at)


def solution(mesh):
    plan = Plan(mesh.shape["vox"], mesh.shape["mem"])
    return jax.shard_map(
        functools.partial(local, plan),
        mesh=mesh,
        in_specs=(
            P("mem", "vox"),
            P("vox", "mem", None),
            P("mem", "vox"),
            P("vox"),
            P("vox"),
            P(("vox", "mem"), None),
            P(("vox", "mem"), None),
            P(),
        ),
        out_specs=P("mem", "vox"),
        check_vma=False,
    )
```

```python
import functools

import jax
import jax.numpy as jnp
from jax import lax
from jax.experimental import pallas as pl
from jax.experimental.pallas import tpu as pltpu
from jax.sharding import PartitionSpec as P

OB = 128
SUB = 8
UNROLL = 8
AXES = ("vox", "mem")
BF = jnp.bfloat16
F32 = jnp.float32


class Plan:
    def __init__(self, nv, nm):
        assert nv % 2 == 0 and nm % nv == 0
        self.nv, self.nm = nv, nm
        self.half, self.inner = nv // 2, nm // nv
        self.chips = nm // 2
        self.everyone = [(v, m) for v in range(nv) for m in range(nm)]

    def device(self, v, q, h):
        x, c = divmod(v, 2)
        qx, qy = divmod(q, self.inner)
        return ((qx + x) % self.half) * 2 + h, (c * self.half + x) * self.inner + qy

    def moved(self, q, i):
        ix, iy = divmod(i, self.inner)
        return ((q // self.inner + ix) % self.half) * self.inner + (q % self.inner + iy) % self.inner

    def flat(self, pairs):
        return [(a * self.nm + b, c * self.nm + d) for (a, b), (c, d) in pairs]

    def out_to_plane(self, i):
        return self.flat([((v, m), self.device(v, self.moved(m // 2, i), m % 2)) for v, m in self.everyone])

    def back(self, i):
        return [(b, a) for a, b in self.out_to_plane(i)]

    def in_plane(self, i):
        return self.flat(
            [
                (self.device(v, q, h), self.device(v, self.moved(q, i), h))
                for v in range(self.nv)
                for q in range(self.chips)
                for h in range(2)
            ]
        )

    def core(self):
        return self.flat([((v, m), (v ^ 1, m)) for v, m in self.everyone])

    def x_shift(self, s):
        return self.flat([((v, m), ((v + 2 * s) % self.nv, m)) for v, m in self.everyone])


def cost(flops, moved):
    return pl.CostEstimate(flops=flops, bytes_accessed=moved, transcendentals=0)


def grant(needed):
    return needed + needed // 8 + (2 << 20)


def vmem(count):
    return [pl.BlockSpec(memory_space=pltpu.VMEM)] * count


def center_kernel(parts, *refs):
    out = refs[parts]
    width = out.shape[1]
    rows = refs[0].shape[0]

    def step(t, carry):
        cols = pl.ds(pl.multiple_of(t * OB, OB), OB)
        values = [r[:, cols].astype(F32) for r in refs[:parts]]
        mean = sum(jnp.sum(x, axis=0, keepdims=True) for x in values) * (1.0 / (parts * rows))
        out[:, cols] = jnp.concatenate([x - mean for x in values], axis=0).astype(BF)
        return carry

    lax.fori_loop(0, width // OB, step, 0, unroll=4)


def center_state(pieces):
    rows, width = pieces[0].shape
    total = rows * len(pieces)
    return pl.pallas_call(
        functools.partial(center_kernel, len(pieces)),
        out_shape=jax.ShapeDtypeStruct((total, width), BF),
        in_specs=vmem(len(pieces)),
        out_specs=vmem(1)[0],
        cost_estimate=cost(4 * total * width, 4 * total * width),
        compiler_params=pltpu.CompilerParams(vmem_limit_bytes=grant(4 * total * width)),
        name="center_state",
    )(*pieces)


def update_kernel(own_parts, *refs):
    n = own_parts
    own, other, pert, state = refs[:n], refs[n : 2 * n], refs[2 * n : 3 * n], refs[3 * n : 4 * n]
    obs, var, kron, anom = refs[4 * n : 4 * n + 4]
    outs = refs[4 * n + 4 : 5 * n + 4]
    stacked, combined = refs[5 * n + 4 :]
    rows = own[0].shape[0]
    count = 2 * n * rows
    lanes = n * rows
    tiles = lanes // SUB
    groups = own[0].shape[1] // OB
    blocks = combined.shape[0]

    def moment(o, carry):
        cols = pl.ds(pl.multiple_of(o * OB, OB), OB)
        mine = jnp.concatenate([r[:, cols].astype(F32) for r in own], axis=0)
        theirs = jnp.concatenate([r[:, cols].astype(F32) for r in other], axis=0)
        noise = jnp.concatenate([r[:, cols].astype(F32) for r in pert], axis=0)
        mean = (jnp.sum(mine, axis=0, keepdims=True) + jnp.sum(theirs, axis=0, keepdims=True)) * (1.0 / count)
        weights = ((obs[:, cols] + noise - mine) * (1.0 / var[:, cols])).astype(BF)
        anomaly = jnp.concatenate([mine - mean, theirs - mean], axis=0).astype(BF)
        m = lax.dot_general(weights, anomaly, (((1,), (1,)), ((), ())), preferred_element_type=F32)
        stacked[:, pl.ds(pl.multiple_of(o * SUB, SUB), SUB), :] = m.reshape(tiles, SUB, count)
        return carry

    lax.fori_loop(0, groups, moment, 0, unroll=UNROLL)

    def combine(g, carry):
        c = lax.dot_general(
            kron[...], stacked[g].astype(BF), (((1,), (0,)), ((), ())), preferred_element_type=F32
        )
        combined[:, pl.ds(pl.multiple_of(g * SUB, SUB), SUB), :] = c.reshape(blocks, SUB, count)
        return carry

    lax.fori_loop(0, tiles, combine, 0, unroll=UNROLL)

    cells = anom.shape[1] // blocks

    def increment(b, carry):
        cols = pl.ds(pl.multiple_of(b * cells, cells), cells)
        inc = lax.dot_general(
            combined[b].astype(BF), anom[:, cols], (((1,), (0,)), ((), ())), preferred_element_type=F32
        )
        for i in range(n):
            new = state[i][:, cols].astype(F32) + inc[i * rows : (i + 1) * rows, :] * (1.0 / (count - 1))
            outs[i][:, cols] = new.astype(BF)
        return carry

    lax.fori_loop(0, blocks, increment, 0, unroll=UNROLL)


def update(own, other, pert, state, obs, var, kron, anom, blocks):
    n = len(own)
    rows, data = own[0].shape
    cells = state[0].shape[1]
    count, lanes = 2 * n * rows, n * rows
    groups = data // OB
    flops = 2 * lanes * count * (data + kron.shape[0] * groups * SUB // SUB + cells)
    held = 2 * (3 * lanes * data + 2 * lanes * cells + count * cells + kron.size) + 64 * data
    held += 4 * lanes * count * (groups + blocks)
    return pl.pallas_call(
        functools.partial(update_kernel, n),
        out_shape=[jax.ShapeDtypeStruct((rows, cells), BF)] * n,
        in_specs=vmem(4 * n + 4),
        out_specs=vmem(n),
        scratch_shapes=[
            pltpu.VMEM((lanes // SUB, groups * SUB, count), F32),
            pltpu.VMEM((blocks, lanes, count), F32),
        ],
        cost_estimate=cost(flops, 2 * (3 * lanes * data + 3 * count * cells)),
        compiler_params=pltpu.CompilerParams(vmem_limit_bytes=grant(held)),
        name="update",
    )(*own, *other, *pert, *state, obs, var, kron, anom)


def place_kernel(parts, at, *refs):
    out, sems = refs[parts], refs[parts + 1]
    width = refs[0].shape[1]
    copies = []
    for i in range(parts):
        start = pl.multiple_of(at[i] * width, OB)
        copies.append(pltpu.make_async_copy(refs[i], out.at[:, pl.ds(start, width)], sems.at[i]))
    for c in copies:
        c.start()
    for c in copies:
        c.wait()


def place(pieces, at):
    n = len(pieces)
    rows, width = pieces[0].shape
    return pl.pallas_call(
        functools.partial(place_kernel, n),
        grid_spec=pltpu.PrefetchScalarGridSpec(
            num_scalar_prefetch=1,
            in_specs=[pl.BlockSpec(memory_space=pl.ANY)] * n,
            out_specs=pl.BlockSpec(memory_space=pl.ANY),
            scratch_shapes=[pltpu.SemaphoreType.DMA((n,))],
        ),
        out_shape=jax.ShapeDtypeStruct((rows, n * width), BF),
        cost_estimate=cost(0, 4 * n * rows * width),
        compiler_params=pltpu.CompilerParams(vmem_limit_bytes=2 << 20),
        name="place",
    )(at, *pieces)


def local(plan, ensemble, partials, perturb, observed, variance, obs_lists, taper_index, taper_table):
    n, half = plan.chips, plan.half
    v, m = lax.axis_index("vox"), lax.axis_index("mem")
    x, core = v // 2, v % 2
    rows, data = perturb.shape
    per_chip = ensemble.shape[1] // n

    def send(value, pairs):
        return lax.ppermute(value, AXES, pairs)

    def chip(i):
        return plan.moved(m // 2, i)

    def part(group_x, group_core):
        return lax.dynamic_slice_in_dim(partials[0], (group_x * 2 + group_core) * data, data, 1)

    away = jnp.concatenate([part(k, 1 - core).astype(BF) for k in range(half)], axis=0)
    got = send(away, plan.core())

    def pair(group_x):
        return part(group_x, core) + lax.dynamic_slice_in_dim(got, group_x * rows, rows, 0).astype(F32)

    total = pair(x)
    for s in range(1, half):
        total = total + send(pair((x + s) % half).astype(BF), plan.x_shift(s)).astype(F32)
    predicted = total.astype(BF)

    groups = data // OB
    table_hits = (
        taper_index[:, :, None] == jnp.arange(taper_table.shape[0], dtype=jnp.int32)[None, None, :]
    ).astype(F32)
    tapers = jnp.sum(table_hits * taper_table[None, None, :], axis=2)
    picks = (obs_lists[:, :, None] == jnp.arange(groups, dtype=jnp.int32)[None, None, :]).astype(F32)
    coeff = jnp.sum(tapers[:, :, None] * picks, axis=1)
    first = plan.out_to_plane(0)
    small = send(jnp.concatenate([observed, variance, coeff.reshape(-1)]), first)
    obs, var = small[:data].reshape(1, data), small[data : 2 * data].reshape(1, data)
    mine = small[2 * data :]
    theirs = send(mine, plan.core())
    blocks = 2 * coeff.shape[0]
    coeff = jnp.where(core == 0, jnp.concatenate([mine, theirs]), jnp.concatenate([theirs, mine]))
    coeff = coeff.reshape(blocks, groups)
    kron = (coeff[:, None, :, None] * jnp.eye(SUB, dtype=F32)[None, :, None, :]).astype(BF)
    kron = kron.reshape(blocks * SUB, groups * SUB)

    def cells_of(q):
        return lax.dynamic_slice_in_dim(ensemble, q * per_chip, per_chip, 1)

    own_state = [send(cells_of(chip(i)), plan.out_to_plane(i)) for i in range(n)]
    other_state = [send(own_state[i], plan.core()) for i in range(n)]
    anom = center_state(own_state + other_state)

    pert = [send(perturb.astype(BF), first)]
    pert += [send(pert[0], plan.in_plane(i)) for i in range(1, n)]
    own = [send(predicted, first)]
    own += [send(own[0], plan.in_plane(i)) for i in range(1, n)]
    other = [send(own[i], plan.core()) for i in range(n)]

    new = update(own, other, pert, own_state, obs, var, kron, anom, blocks)
    back = [send(new[i], plan.back(i)) for i in range(n)]
    at = jnp.stack([chip(i) for i in range(n)]).astype(jnp.int32)
    return place(back, at)


def whole(plan, *args):
    return local(plan, *args)


def solution(mesh):
    plan = Plan(mesh.shape["vox"], mesh.shape["mem"])
    return jax.shard_map(
        functools.partial(whole, plan),
        mesh=mesh,
        in_specs=(
            P("mem", "vox"),
            P("vox", "mem", None),
            P("mem", "vox"),
            P("vox"),
            P("vox"),
            P(("vox", "mem"), None),
            P(("vox", "mem"), None),
            P(),
        ),
        out_specs=P("mem", "vox"),
        check_vma=False,
    )
```
